256 devices in a mesh: query: 4 (over y), context: 64 (over x, z, core).
Axes of the slice: x: 4, y: 4, z: 8, core: 2. Of those that a mesh axis runs over, the one named last changes fastest.
Arguments:
- queries: bfloat16 [4, 8192, 128], P('query', 'context'), may hold values from -6 to 6
- keys: bfloat16 [8192, 128], P('context'), may hold values from -6 to 6
- values: bfloat16 [8192, 128], P('context'), may hold values from -6 to 6
- out_grad: bfloat16 [4, 8192, 128], P('query', 'context'), may hold values from -6 to 6
- prefix_states: bfloat16 [64, 8256, 128], P('context'), may hold values from -48 to 48
Outputs:
- grad_queries: bfloat16 [4, 8192, 128], P('query', 'context')
- grad_keys: bfloat16 [64, 128, 128], P('context', 'query')
- grad_values: bfloat16 [64, 128, 128], P('context', 'query')
The draws below stay inside these ranges and needn't reach their ends.
All inputs are finite; a program needn't handle non-finite values.
Results may differ from the reference program's by a relative error of at most 0.014.
Values may be sent and summed in bfloat16 or wider, within the bound.
No kernel may reach another device: no remote copies, remote signals or barrier semaphores. Data moves between devices by JAX's collectives and lax.ppermute only.
A program may use at most 192 MiB of HBM per device.

```python
import jax
import jax.numpy as jnp
import numpy as np
from jax import lax

D = 128
TOK_DEV = 128
FEATURES = 8256
HEADS = 4
BLOCKS = 64
TOKENS = 8192


def level_of(rng, shape, shards, smallest, top_value):
    factor_of, own = 1.0, jax.random.fold_in(rng, 6)
    for axis_at, parts in shards:
        steps = jnp.exp(jax.random.uniform(jax.random.fold_in(own, axis_at), (parts,), jnp.float32, smallest / len(shards), top_value / len(shards)))
        factor_of = factor_of * jnp.repeat(steps, shape[axis_at] // parts).reshape([-1 if axis == axis_at else 1 for axis in range(len(shape))])
    return factor_of


def centred(rng, shape, spread, bound, shards=(), held_as=jnp.bfloat16):
    array = spread * jax.random.normal(rng, shape, jnp.float32)
    if shards:
        array = array * level_of(rng, shape, shards, -0.22, 0.18)
    return jnp.clip(array, -bound, bound).astype(held_as)


def setup_inputs(seed: int = 0) -> dict:
    key_of = jax.random.split(jax.random.key(seed), 6)
    queries = centred(key_of[0], (HEADS, TOKENS, D), 1.0, 6.0, ((0, 4), (1, 64)))
    keys = centred(key_of[1], (TOKENS, D), 1.0, 6.0, ((0, 64),))
    values = centred(key_of[2], (TOKENS, D), 1.0, 6.0, ((0, 64),))
    out_grad = centred(key_of[3], (HEADS, TOKENS, D), 1.0, 6.0, ((0, 4), (1, 64)))
    prefix_states = centred(key_of[4], (BLOCKS, FEATURES, D), (TOK_DEV // 16), 48.0, ((0, 64),))
    return {"queries": queries, "keys": keys, "values": values, "out_grad": out_grad, "prefix_states": prefix_states}


def pair_tables(model_width):
    first_index, second_index = np.triu_indices(model_width)
    pair_weight = np.where(first_index == second_index, 1.0, np.sqrt(2.0)).astype(np.float32)
    return (first_index.astype(np.int32), second_index.astype(np.int32), pair_weight)

def expand_rows(rows_in, first_index, second_index, pair_weight):
    column_form = rows_in.astype(jnp.float32).T
    return (column_form[first_index] * column_form[second_index] * pair_weight[:, None]).astype(jnp.bfloat16)

def pair_grad(feature_grad, column_form, first_index, second_index, pair_weight, onehot_first, onehot_second):
    weighted = feature_grad.astype(jnp.float32) * pair_weight[:, None]
    term_one = (weighted * column_form[second_index]).astype(jnp.bfloat16)
    term_two = (weighted * column_form[first_index]).astype(jnp.bfloat16)
    dims = (((0,), (0,)), ((), ()))
    return lax.dot_general(term_one, onehot_first, dims, preferred_element_type=jnp.float32) + lax.dot_general(term_two, onehot_second, dims, preferred_element_type=jnp.float32)

def reference(queries, keys, values, out_grad, prefix_states):
    head_count, token_count, model_width = queries.shape
    block_count = prefix_states.shape[0]
    row_count = token_count // block_count
    score_scale = 1.0 / (model_width * row_count)
    first_index, second_index, pair_weight = pair_tables(model_width)
    width_range = jnp.arange(model_width, dtype=jnp.int32)
    onehot_first = (jnp.asarray(first_index)[:, None] == width_range[None, :]).astype(jnp.bfloat16)
    onehot_second = (jnp.asarray(second_index)[:, None] == width_range[None, :]).astype(jnp.bfloat16)
    query_blocks = queries.reshape(head_count, block_count, row_count, model_width)
    grad_blocks = out_grad.reshape(head_count, block_count, row_count, model_width)
    key_blocks = keys.reshape(block_count, row_count, model_width)
    value_blocks = values.reshape(block_count, row_count, model_width)

    def block_state(index):
        total = jnp.zeros((first_index.shape[0], model_width), jnp.float32)
        for head_index in range(head_count):
            expanded = expand_rows(query_blocks[head_index, index], first_index, second_index, pair_weight)
            total = total + jnp.dot(expanded, grad_blocks[head_index, index], preferred_element_type=jnp.float32)
        return score_scale * total
    states = lax.map(block_state, jnp.arange(block_count, dtype=jnp.int32))
    later = jnp.cumsum(states[::-1], axis=0)[::-1]
    suffix = jnp.concatenate([later[1:], jnp.zeros_like(later[:1])], axis=0)
    causal = jnp.arange(row_count)[None, :] <= jnp.arange(row_count)[:, None]

    def block_grads(index):
        key_rows = key_blocks[index]
        value_rows = value_blocks[index]
        grad_state = suffix[index].astype(jnp.bfloat16)
        prefix = prefix_states[index]
        key_cols = key_rows.astype(jnp.float32).T
        expanded_keys = expand_rows(key_rows, first_index, second_index, pair_weight)
        value_sum = jnp.dot(expanded_keys.T, grad_state, preferred_element_type=jnp.float32)
        key_feature = jnp.dot(grad_state, value_rows.T, preferred_element_type=jnp.float32).astype(jnp.bfloat16)
        key_sum = pair_grad(key_feature, key_cols, first_index, second_index, pair_weight, onehot_first, onehot_second)
        query_list = []
        for head_index in range(head_count):
            query_rows = query_blocks[head_index, index]
            grad_rows = grad_blocks[head_index, index]
            score_dot = jnp.dot(query_rows, key_rows.T, preferred_element_type=jnp.float32)
            grad_dot = jnp.dot(grad_rows, value_rows.T, preferred_element_type=jnp.float32)
            attn = jnp.where(causal, score_scale * score_dot * score_dot, 0.0).astype(jnp.bfloat16)
            slope = jnp.where(causal, 2.0 * score_scale * score_dot * grad_dot, 0.0).astype(jnp.bfloat16)
            local_query = jnp.dot(slope, key_rows, preferred_element_type=jnp.float32)
            key_sum = key_sum + jnp.dot(slope.T, query_rows, preferred_element_type=jnp.float32)
            value_sum = value_sum + jnp.dot(attn.T, grad_rows, preferred_element_type=jnp.float32)
            query_feature = jnp.dot(prefix, grad_rows.T, preferred_element_type=jnp.float32).astype(jnp.bfloat16)
            cross_query = score_scale * pair_grad(query_feature, query_rows.astype(jnp.float32).T, first_index, second_index, pair_weight, onehot_first, onehot_second)
            query_list.append((local_query + cross_query).astype(jnp.bfloat16))
        return (jnp.stack(query_list), key_sum.astype(jnp.bfloat16), value_sum.astype(jnp.bfloat16))
    grad_q, grad_k, grad_v = lax.map(block_grads, jnp.arange(block_count, dtype=jnp.int32))
    grad_q = grad_q.transpose(1, 0, 2, 3).reshape(head_count, token_count, model_width)
    return (grad_q, grad_k, grad_v)
```

```python
import functools

import jax
import jax.numpy as jnp
import numpy as np
from jax import lax
from jax.experimental import pallas as pl
from jax.experimental.pallas import tpu as pltpu
from jax.sharding import Mesh, PartitionSpec as P

X_SIZE = 4
Z_SIZE = 8
C_SIZE = 2

NT_DIMS = (((1,), (1,)), ((), ()))
TN_DIMS = (((0,), (0,)), ((), ()))


def dot(a, b, dims=(((1,), (0,)), ((), ()))):
    return lax.dot_general(a, b, dims, preferred_element_type=jnp.float32)


def local_kernel(scale, q_ref, g_ref, k_ref, v_ref, p_ref, gq_ref, pair_ref, feat, x_cols, part):
    d = q_ref.shape[1]
    rows = q_ref.shape[0]
    q, g, k, v = q_ref[...], g_ref[...], k_ref[...], v_ref[...]
    score = dot(k, q, NT_DIMS)
    grad = dot(v, g, NT_DIMS)
    s_at = lax.broadcasted_iota(jnp.int32, (rows, rows), 0)
    t_at = lax.broadcasted_iota(jnp.int32, (rows, rows), 1)
    causal = s_at <= t_at
    attn = jnp.where(causal, scale * score * score, 0.0).astype(jnp.bfloat16)
    slope = jnp.where(causal, 2.0 * scale * score * grad, 0.0).astype(jnp.bfloat16)
    pair_ref[:, :d] = dot(slope, q)
    pair_ref[:, d:] = dot(attn, g)
    features = p_ref.shape[0]
    chunk = 688
    for at in range(0, features, chunk):
        feat[at : at + chunk, :] = dot(p_ref[at : at + chunk, :], g, NT_DIMS)
    x_cols[...] = q.astype(jnp.float32).T
    sub = lax.broadcasted_iota(jnp.int32, (8, rows), 0)
    root_half = np.float32(np.sqrt(0.5))
    diag = [
        jnp.where(sub > r, np.float32(1.0), jnp.where(sub == r, root_half, np.float32(0.0)))
        for r in range(8)
    ]
    second = [jnp.zeros((8, rows), jnp.float32) for _ in range(d // 8)]
    offset = 0
    for i in range(d):
        base = offset - i
        x_i = jnp.broadcast_to(x_cols[i : i + 1, :], (8, rows))
        first = None
        for m in range(i // 8, d // 8):
            if m == i // 8:
                lo = base + 8 * m
                if lo < 0:
                    lo = 0
                f = feat[lo : lo + 8, :] * diag[i % 8]
            else:
                f = feat[base + 8 * m : base + 8 * m + 8, :]
            term = f * x_cols[8 * m : 8 * m + 8, :]
            first = term if first is None else first + term
            second[m] = second[m] + f * x_i
        part[8 * i : 8 * i + 8, :] = first
        offset += d - i
    for m in range(d // 8):
        total = second[m]
        for r in range(8):
            total = total + part[pl.ds(64 * m + r, 8, stride=8), :]
        x_cols[8 * m : 8 * m + 8, :] = total
    cross = np.float32(np.sqrt(2.0) * scale) * x_cols[...].T
    gq_ref[...] = (dot(slope, k, TN_DIMS) + cross).astype(jnp.bfloat16)


def add_later(scale, places, tokens_ref, keys_ref, acc, at_t, at_s):
    d = keys_ref.shape[2] // 2
    groups, rows = keys_ref.shape[0], keys_ref.shape[1]
    k = keys_ref[:, :, :d].reshape(groups * rows, d)
    v = keys_ref[:, :, d:].reshape(groups * rows, d)
    width = 2 * rows
    lane = lax.broadcasted_iota(jnp.int32, (1, width), 1)
    for n in range(tokens_ref.shape[0] // 2):
        q = tokens_ref[2 * n : 2 * n + 2, :, :d].reshape(width, d)
        g = tokens_ref[2 * n : 2 * n + 2, :, d:].reshape(width, d)
        score = dot(k, q, NT_DIMS)
        grad = dot(v, g, NT_DIMS)
        block = at_t + 2 * (2 * n + jnp.where(lane >= rows, 1, 0))
        attn, slope = [], []
        for j in range(groups):
            c = jnp.where(block > at_s + places * j, np.float32(scale), np.float32(0.0))
            s = score[rows * j : rows * (j + 1), :]
            cs = c * s
            attn.append((cs * s).astype(jnp.bfloat16))
            slope.append((cs * 2.0 * grad[rows * j : rows * (j + 1), :]).astype(jnp.bfloat16))
        acc[:, :d] += dot(jnp.concatenate(slope, axis=0), q)
        acc[:, d:] += dot(jnp.concatenate(attn, axis=0), g)


def first_kernel(scale, places, where_ref, tokens_ref, keys_ref, pair_ref, acc_ref):
    rows = keys_ref.shape[1]
    own = where_ref[0]
    for j in range(keys_ref.shape[0]):
        keep = jnp.where(own == j, np.float32(1.0), np.float32(0.0))
        acc_ref[rows * j : rows * (j + 1), :] = pair_ref[...] * keep
    add_later(scale, places, tokens_ref, keys_ref, acc_ref, where_ref[1], where_ref[3])


def second_kernel(scale, places, where_ref, tokens_ref, keys_ref, in_ref, out_ref, acc):
    acc[...] = in_ref[...]
    add_later(scale, places, tokens_ref, keys_ref, acc, where_ref[2], where_ref[3])
    heads, groups, share = out_ref.shape[0], out_ref.shape[1], out_ref.shape[2]
    rows = keys_ref.shape[1]
    for j in range(groups):
        for h in range(heads):
            at = rows * j + share * h
            out_ref[h, j, :, :] = acc[at : at + share, :].astype(jnp.bfloat16)


def body(queries, keys, values, out_grad, prefix_states):
    q, g, p = queries[0], out_grad[0], prefix_states[0]
    rows, d = q.shape
    scale = 1.0 / (d * rows)
    heads = lax.axis_size("query")
    groups = lax.axis_size("x")
    depth = lax.axis_size("z")
    places = depth * lax.axis_size("c")
    x_at, z_at, c_at = lax.axis_index("x"), lax.axis_index("z"), lax.axis_index("c")
    vmem = pl.BlockSpec(memory_space=pltpu.VMEM)
    smem = pl.BlockSpec(memory_space=pltpu.SMEM)

    key_pair = jnp.concatenate([keys, values], axis=1)
    query_pair = jnp.concatenate([q, g], axis=1)
    keys_all = lax.all_to_all(jnp.broadcast_to(key_pair[None], (groups, rows, 2 * d)), "x", 0, 0)
    tokens = lax.all_to_all(jnp.broadcast_to(query_pair[None], (depth, rows, 2 * d)), "z", 0, 0)
    tokens_other = lax.ppermute(tokens, "c", [(0, 1), (1, 0)])

    grad_queries, pair = pl.pallas_call(
        functools.partial(local_kernel, scale),
        out_shape=(
            jax.ShapeDtypeStruct((rows, d), jnp.bfloat16),
            jax.ShapeDtypeStruct((rows, 2 * d), jnp.float32),
        ),
        in_specs=[vmem] * 5,
        out_specs=(vmem, vmem),
        scratch_shapes=[
            pltpu.VMEM(p.shape, jnp.float32),
            pltpu.VMEM((d, rows), jnp.float32),
            pltpu.VMEM((8 * d, rows), jnp.float32),
        ],
        name="local",
    )(q, g, keys, values, p)

    where = jnp.stack(
        [x_at, x_at * places + c_at, x_at * places + 1 - c_at, 2 * z_at + c_at]
    ).astype(jnp.int32)
    acc = pl.pallas_call(
        functools.partial(first_kernel, scale, places),
        out_shape=jax.ShapeDtypeStruct((groups * rows, 2 * d), jnp.float32),
        in_specs=[smem, vmem, vmem, vmem],
        out_specs=vmem,
        name="first_half",
    )(where, tokens, keys_all, pair)
    pieces = pl.pallas_call(
        functools.partial(second_kernel, scale, places),
        out_shape=jax.ShapeDtypeStruct((heads, groups, rows // heads, 2 * d), jnp.bfloat16),
        in_specs=[smem, vmem, vmem, vmem],
        out_specs=vmem,
        scratch_shapes=[pltpu.VMEM((groups * rows, 2 * d), jnp.float32)],
        name="second_half",
    )(where, tokens_other, keys_all, acc)
    pieces = pieces.reshape(heads * groups, rows // heads, 2 * d)
    arrived = lax.all_to_all(pieces, ("query", "x"), 0, 0)
    total = jnp.sum(arrived.astype(jnp.float32), axis=0)
    grad_keys = total[:, :d].astype(jnp.bfloat16)[None]
    grad_values = total[:, d:].astype(jnp.bfloat16)[None]
    return (grad_queries[None], grad_keys, grad_values)


def solution(mesh):
    split = Mesh(
        mesh.devices.reshape(mesh.shape["query"], X_SIZE, Z_SIZE, C_SIZE),
        ("query", "x", "z", "c"),
    )
    context = ("x", "z", "c")
    return jax.shard_map(
        body,
        mesh=split,
        in_specs=(
            P("query", context, None),
            P(context, None),
            P(context, None),
            P("query", context, None),
            P(context, None, None),
        ),
        out_specs=(
            P("query", context, None),
            P(context, "query", None),
            P(context, "query", None),
        ),
        check_vma=False,
    )
```

```python
import functools

import jax
import jax.numpy as jnp
import numpy as np
from jax import lax
from jax.experimental import pallas as pl
from jax.experimental.pallas import tpu as pltpu
from jax.sharding import Mesh, PartitionSpec as P

X_SIZE = 4
Z_SIZE = 8
C_SIZE = 2

NT_DIMS = (((1,), (1,)), ((), ()))
TN_DIMS = (((0,), (0,)), ((), ()))


def dot(a, b, dims=(((1,), (0,)), ((), ()))):
    return lax.dot_general(a, b, dims, preferred_element_type=jnp.float32)


def local_kernel(scale, q_ref, g_ref, k_ref, v_ref, p_ref, gq_ref, pair_ref, feat, x_cols, part):
    d = q_ref.shape[1]
    rows = q_ref.shape[0]
    q, g, k, v = q_ref[...], g_ref[...], k_ref[...], v_ref[...]
    score = dot(k, q, NT_DIMS)
    grad = dot(v, g, NT_DIMS)
    s_at = lax.broadcasted_iota(jnp.int32, (rows, rows), 0)
    t_at = lax.broadcasted_iota(jnp.int32, (rows, rows), 1)
    causal = s_at <= t_at
    attn = jnp.where(causal, scale * score * score, 0.0).astype(jnp.bfloat16)
    slope = jnp.where(causal, 2.0 * scale * score * grad, 0.0).astype(jnp.bfloat16)
    pair_ref[:, :d] = dot(slope, q)
    pair_ref[:, d:] = dot(attn, g)
    features = p_ref.shape[0]
    chunk = 688
    for at in range(0, features, chunk):
        feat[at : at + chunk, :] = dot(p_ref[at : at + chunk, :], g, NT_DIMS)
    x_cols[...] = q.astype(jnp.float32).T
    sub = lax.broadcasted_iota(jnp.int32, (8, rows), 0)
    root_half = np.float32(np.sqrt(0.5))
    diag = [
        jnp.where(sub > r, np.float32(1.0), jnp.where(sub == r, root_half, np.float32(0.0)))
        for r in range(8)
    ]
    second = [jnp.zeros((8, rows), jnp.float32) for _ in range(d // 8)]
    offset = 0
    for i in range(d):
        base = offset - i
        x_i = jnp.broadcast_to(x_cols[i : i + 1, :], (8, rows))
        first = None
        for m in range(i // 8, d // 8):
            if m == i // 8:
                lo = base + 8 * m
                if lo < 0:
                    lo = 0
                f = feat[lo : lo + 8, :] * diag[i % 8]
            else:
                f = feat[base + 8 * m : base + 8 * m + 8, :]
            term = f * x_cols[8 * m : 8 * m + 8, :]
            first = term if first is None else first + term
            second[m] = second[m] + f * x_i
        part[8 * i : 8 * i + 8, :] = first
        offset += d - i
    for m in range(d // 8):
        total = second[m]
        for r in range(8):
            total = total + part[pl.ds(64 * m + r, 8, stride=8), :]
        x_cols[8 * m : 8 * m + 8, :] = total
    cross = np.float32(np.sqrt(2.0) * scale) * x_cols[...].T
    gq_ref[...] = (dot(slope, k, TN_DIMS) + cross).astype(jnp.bfloat16)


def copies_kernel(q_ref, g_ref, k_ref, v_ref, tokens_ref, keys_ref):
    d = q_ref.shape[1]
    for n in range(tokens_ref.shape[0]):
        tokens_ref[n, :, :d] = q_ref[...]
        tokens_ref[n, :, d:] = g_ref[...]
    keys_ref[:, :d] = k_ref[...]
    keys_ref[:, d:] = v_ref[...]


def add_later(scale, tokens_ref, key_refs, acc, own, step):
    rows, d = key_refs[0].shape[0], key_refs[0].shape[1] // 2
    k = jnp.concatenate([ref[:, :d] for ref in key_refs], axis=0)
    v = jnp.concatenate([ref[:, d:] for ref in key_refs], axis=0)
    width = 2 * rows
    lane = lax.broadcasted_iota(jnp.int32, (1, width), 1)
    for n in range(tokens_ref.shape[0] // 2):
        q = tokens_ref[2 * n : 2 * n + 2, :, :d].reshape(width, d)
        g = tokens_ref[2 * n : 2 * n + 2, :, d:].reshape(width, d)
        score = dot(k, q, NT_DIMS)
        grad = dot(v, g, NT_DIMS)
        ahead = 2 * (2 * n + jnp.where(lane >= rows, 1, 0)) - own
        attn, slope = [], []
        for j in range(len(key_refs)):
            c = jnp.where(ahead + step * j > 0, np.float32(scale), np.float32(0.0))
            s = score[rows * j : rows * (j + 1), :]
            cs = c * s
            attn.append((cs * s).astype(jnp.bfloat16))
            slope.append((cs * 2.0 * grad[rows * j : rows * (j + 1), :]).astype(jnp.bfloat16))
        acc[:, :d] += dot(jnp.concatenate(slope, axis=0), q)
        acc[:, d:] += dot(jnp.concatenate(attn, axis=0), g)


def first_kernel(scale, step, tokens_ref, *refs):
    key_refs, pair_ref, acc_ref = refs[:-2], refs[-2], refs[-1]
    rows = pair_ref.shape[0]
    acc_ref[:rows, :] = pair_ref[...]
    acc_ref[rows:, :] = jnp.zeros_like(acc_ref[rows:, :])
    add_later(scale, tokens_ref, key_refs, acc_ref, 2 * lax.axis_index("z"), step)


def second_kernel(scale, step, tokens_ref, *refs):
    key_refs, in_ref, out_ref, acc = refs[:-3], refs[-3], refs[-2], refs[-1]
    acc[...] = in_ref[...]
    own = 2 * lax.axis_index("z") + 2 * lax.axis_index("c") - 1
    add_later(scale, tokens_ref, key_refs, acc, own, step)
    heads, groups, share = out_ref.shape[0], out_ref.shape[1], out_ref.shape[2]
    rows = key_refs[0].shape[0]
    for j in range(groups):
        to = lax.rem(lax.axis_index("x") - j + groups, groups)
        for h in range(heads):
            at = rows * j + share * h
            out_ref[h, to, :, :] = acc[at : at + share, :].astype(jnp.bfloat16)


def body(queries, keys, values, out_grad, prefix_states):
    q, g, p = queries[0], out_grad[0], prefix_states[0]
    rows, d = q.shape
    scale = 1.0 / (d * rows)
    heads = lax.axis_size("query")
    groups = lax.axis_size("x")
    depth = lax.axis_size("z")
    places = depth * lax.axis_size("c")
    vmem = pl.BlockSpec(memory_space=pltpu.VMEM)

    token_copies, key_pair = pl.pallas_call(
        copies_kernel,
        out_shape=(
            pltpu.VMEM((depth, rows, 2 * d), jnp.bfloat16),
            pltpu.VMEM((rows, 2 * d), jnp.bfloat16),
        ),
        in_specs=[vmem] * 4,
        out_specs=(vmem, vmem),
        name="copies",
    )(q, g, keys, values)
    tokens = lax.all_to_all(token_copies, "z", 0, 0)
    keys_all = [key_pair] + [
        lax.ppermute(key_pair, "x", [(i, i + j) for i in range(groups - j)])
        for j in range(1, groups)
    ]

    grad_queries, pair = pl.pallas_call(
        functools.partial(local_kernel, scale),
        out_shape=(
            jax.ShapeDtypeStruct((rows, d), jnp.bfloat16),
            pltpu.VMEM((rows, 2 * d), jnp.float32),
        ),
        in_specs=[vmem] * 5,
        out_specs=(vmem, vmem),
        scratch_shapes=[
            pltpu.VMEM(p.shape, jnp.float32),
            pltpu.VMEM((d, rows), jnp.float32),
            pltpu.VMEM((8 * d, rows), jnp.float32),
        ],
        name="local",
    )(q, g, keys, values, p)

    tokens, keys_all, grad_queries, pair = lax.optimization_barrier(
        (tokens, keys_all, grad_queries, pair)
    )
    tokens_other = lax.ppermute(tokens, "c", [(0, 1), (1, 0)])

    near = functools.partial(pltpu.with_memory_space_constraint, memory_space=pltpu.VMEM)
    keys_all = [near(block) for block in keys_all]
    acc = pl.pallas_call(
        functools.partial(first_kernel, scale, places),
        out_shape=pltpu.VMEM((groups * rows, 2 * d), jnp.float32),
        in_specs=[vmem] * (groups + 2),
        out_specs=vmem,
        name="first_half",
    )(near(tokens), *keys_all, near(pair))
    pieces = pl.pallas_call(
        functools.partial(second_kernel, scale, places),
        out_shape=pltpu.VMEM((heads, groups, rows // heads, 2 * d), jnp.bfloat16),
        in_specs=[vmem] * (groups + 2),
        out_specs=vmem,
        scratch_shapes=[pltpu.VMEM((groups * rows, 2 * d), jnp.float32)],
        name="second_half",
    )(near(tokens_other), *keys_all, near(acc))
    pieces = pieces.reshape(heads * groups, rows // heads, 2 * d)
    arrived = lax.all_to_all(pieces, ("query", "x"), 0, 0)
    total = jnp.sum(arrived.astype(jnp.float32), axis=0)
    grad_keys = total[:, :d].astype(jnp.bfloat16)[None]
    grad_values = total[:, d:].astype(jnp.bfloat16)[None]
    return (grad_queries[None], grad_keys, grad_values)


def solution(mesh):
    split = Mesh(
        mesh.devices.reshape(mesh.shape["query"], X_SIZE, Z_SIZE, C_SIZE),
        ("query", "x", "z", "c"),
    )
    context = ("x", "z", "c")
    return jax.shard_map(
        body,
        mesh=split,
        in_specs=(
            P("query", context, None),
            P(context, None),
            P(context, None),
            P("query", context, None),
            P(context, None, None),
        ),
        out_specs=(
            P("query", context, None),
            P(context, "query", None),
            P(context, "query", None),
        ),
        check_vma=False,
    )
```
